128 devices in a mesh: aux: 64 (over y, z_hi, x, core), ao: 2 (over z_lo).
Axes of the slice: x: 4, y: 4, z: 4 (z_hi: 2, z_lo: 2; z = z_hi * 2 + z_lo), core: 2. Of those that a mesh axis runs over, the one named last changes fastest.
Arguments:
- ints: bfloat16 [1024, 768, 768], P('aux', 'ao'), may hold values from -1.25 to 1.25
- occ_coef: bfloat16 [768, 128], replicated, may hold values from -0.21875 to 0.21875
- vir_coef: bfloat16 [768, 512], P('ao'), may hold values from -0.21875 to 0.21875
- occ_energy: float32 [128], replicated, may hold values from -2 to -0.3
- vir_energy: float32 [512], replicated, may hold values from 0.3 to 3
Outputs:
- density: float32 [128, 512, 512], P('aux', 'ao')
The draws below stay inside these ranges and needn't reach their ends.
All inputs are finite; a program needn't handle non-finite values.
Results may differ from the reference program's by a relative error of at most 0.0065.
Values may be sent and summed in bfloat16 or wider, within the bound.
No kernel may reach another device: no remote copies, remote signals or barrier semaphores. Data moves between devices by JAX's collectives and lax.ppermute only.
A program may use at most 128 MiB of HBM per device.

```python
import jax
import jax.numpy as jnp
from jax import lax

AO = 768
NVIR = 512
OCC_DEV = 2
CYCLE = 4
NOCC = 128
NAUX = 1024
N_AUX = 64


def block_scale(stream_key, extent, pieces, least, top_value):
    gain, own = 1.0, jax.random.fold_in(stream_key, 6)
    for axis_at, blocks in pieces:
        heights = jnp.exp(jax.random.uniform(jax.random.fold_in(own, axis_at), (blocks,), jnp.float32, least / len(pieces), top_value / len(pieces)))
        gain = gain * jnp.repeat(heights, extent[axis_at] // blocks).reshape([-1 if axis == axis_at else 1 for axis in range(len(extent))])
    return gain


def centred(own_key, dims, width, bound, cuts=(), held_as=jnp.bfloat16):
    level = block_scale(own_key, dims, cuts, -0.22, 0.18) if cuts else 1.0
    drawn = jax.random.normal(own_key, dims, jnp.float32) * width * level
    return jnp.minimum(jnp.maximum(drawn, -bound), bound).astype(held_as)


def setup_inputs(seed: int = 0) -> dict:
    key_list = jax.random.split(jax.random.key(seed), 6)
    ints = centred(key_list[0], (NAUX, AO, AO), 0.08, 1.25, ((0, 64), (1, 2)))
    occ_coef = centred(key_list[1], (AO, NOCC), AO ** -0.5, 0.21875)
    vir_coef = centred(key_list[2], (AO, NVIR), AO ** -0.5, 0.21875, ((0, 2),))
    occ_energy = jnp.clip(jax.random.uniform(key_list[3], (NOCC,), jnp.float32, -2.0, -0.3), -2.0, -0.3)
    vir_energy = jnp.clip(jax.random.uniform(key_list[4], (NVIR,), jnp.float32, 0.3, 3.0), 0.3, 3.0)
    return {"ints": ints, "occ_coef": occ_coef, "vir_coef": vir_coef, "occ_energy": occ_energy, "vir_energy": vir_energy}


def reference(ints, occ_coef, vir_coef, occ_energy, vir_energy):
    def transform(slab):
        half_ints = jnp.dot(slab, occ_coef, preferred_element_type=jnp.float32).astype(jnp.bfloat16)
        return jnp.dot(half_ints.T, vir_coef, preferred_element_type=jnp.float32).astype(jnp.bfloat16)

    three = lax.map(transform, ints)
    offsets = jnp.arange(2 * CYCLE + 1, dtype=jnp.int32) - CYCLE
    inside = jnp.arange(OCC_DEV, dtype=jnp.int32)
    vir_pairs = vir_energy[:, None] + vir_energy[None, :]

    def one_orbital(orbital):
        block_index = orbital // OCC_DEV
        blocks = (block_index + offsets + N_AUX) % N_AUX
        partners = (blocks[:, None] * OCC_DEV + inside[None, :]).reshape(-1).astype(jnp.int32)
        partner_rows = jnp.take(three, partners, axis=1).astype(jnp.float32)
        own_rows = lax.dynamic_index_in_dim(three, orbital, 1, keepdims=False).astype(jnp.float32)
        integrals = jnp.einsum("qa,qjb->jab", own_rows, partner_rows)
        own_energy = lax.dynamic_index_in_dim(occ_energy, orbital, 0, keepdims=False)
        pair_energy = jnp.take(occ_energy, partners, axis=0)
        energy_gap = own_energy + pair_energy[:, None, None] - vir_pairs[None]
        scaled = integrals / energy_gap
        amplitude = scaled.astype(jnp.bfloat16).astype(jnp.float32)
        mixed = (2.0 * scaled - jnp.swapaxes(scaled, 1, 2)).astype(jnp.bfloat16).astype(jnp.float32)
        return jnp.einsum("jac,jbc->ab", amplitude, mixed)

    return lax.map(one_orbital, jnp.arange(NOCC, dtype=jnp.int32))
```

```python
import jax
import jax.numpy as jnp
from jax import lax
from jax.experimental import pallas as pl
from jax.experimental.pallas import tpu as pltpu
from jax.sharding import PartitionSpec as P

CYCLE = 4
ROW = 8
LANES = 128
BOTH = ("aux", "ao")
VMEM_LIMIT = 56 * 1024 * 1024


def flipped(block):
    return (block // ROW) % 2


def transform_kernel(slots, ints_ref, occ_ref, vir_ref, out_ref, held_ref):
    step = pl.program_id(0)
    chunk, rows, width = ints_ref.shape
    nocc = occ_ref.shape[1]
    slab = ints_ref[...].reshape(chunk * rows, width)
    half = jnp.dot(slab, occ_ref[...], preferred_element_type=jnp.float32).astype(jnp.bfloat16)
    for k in range(chunk):
        part = lax.dot_general(
            half[k * rows : (k + 1) * rows],
            vir_ref[...],
            (((0,), (0,)), ((), ())),
            preferred_element_type=jnp.float32,
        )
        start = pl.multiple_of((step * chunk + k) * nocc, nocc)
        for column in range(0, part.shape[1], LANES):
            row = column // LANES * (held_ref.shape[0] * LANES // part.shape[1])
            held_ref[pl.ds(row + start, nocc), :] = part[:, column : column + LANES]

    @pl.when(step == pl.num_programs(0) - 1)
    def _():
        count, nvir = out_ref.shape[1:]
        for orbital in range(nocc):
            for column in range(0, nvir, LANES):
                row = column // LANES * count * nocc + orbital
                tile = held_ref[pl.ds(row, count, stride=nocc), :]
                out_ref[slots[orbital], :, column : column + LANES] = tile.astype(jnp.bfloat16)


def transform(ints, occ_coef, vir_coef, slots, chunk=4):
    count, rows, width = ints.shape
    nocc, nvir = occ_coef.shape[1], vir_coef.shape[1]
    return pl.pallas_call(
        lambda *refs: transform_kernel(slots, *refs),
        grid=(count // chunk,),
        in_specs=[
            pl.BlockSpec((chunk, rows, width), lambda s: (s, 0, 0)),
            pl.BlockSpec((width, nocc), lambda s: (0, 0)),
            pl.BlockSpec((rows, nvir), lambda s: (0, 0)),
        ],
        out_specs=pl.BlockSpec((nocc, count, nvir), lambda s: (0, 0, 0)),
        out_shape=jax.ShapeDtypeStruct((nocc, count, nvir), jnp.bfloat16),
        scratch_shapes=[pltpu.VMEM((count * nocc * nvir // LANES, LANES), jnp.float32)],
        compiler_params=pltpu.CompilerParams(vmem_limit_bytes=VMEM_LIMIT),
        name="transform",
    )(ints, occ_coef, vir_coef)


def combine_kernel(in_ref, own_ref, turned_ref):
    tiles = in_ref[...].astype(jnp.float32)
    total = tiles[:, 0] + tiles[:, 1]
    total = total.reshape(own_ref.shape)
    own_ref[...] = total.astype(jnp.bfloat16)
    turned_ref[...] = total.T.astype(jnp.bfloat16)


def combine(arrived, chunk=16):
    owners, halves, count, nvir = arrived.shape
    naux = owners * count
    return pl.pallas_call(
        combine_kernel,
        grid=(owners // chunk,),
        in_specs=[pl.BlockSpec((chunk, halves, count, nvir), lambda s: (s, 0, 0, 0))],
        out_specs=[
            pl.BlockSpec((chunk * count, nvir), lambda s: (s, 0)),
            pl.BlockSpec((nvir, chunk * count), lambda s: (0, s)),
        ],
        out_shape=[
            jax.ShapeDtypeStruct((naux, nvir), jnp.bfloat16),
            jax.ShapeDtypeStruct((nvir, naux), jnp.bfloat16),
        ],
        compiler_params=pltpu.CompilerParams(vmem_limit_bytes=VMEM_LIMIT),
        name="combine",
    )(arrived)


def pair_kernel(visitors, energy_ref, column_ref, row_ref, turned_ref, *refs):
    visitor_refs, rest = refs[:visitors], refs[visitors:]
    out_ref = rest[-1]
    vir_pairs = column_ref[...] + row_ref[...]
    total = rest[0][...] if len(rest) > 1 else None
    for k in range(visitors):
        integrals = jnp.dot(
            turned_ref[...], visitor_refs[k][...], preferred_element_type=jnp.float32
        )
        scaled = integrals / (energy_ref[k] - vir_pairs)
        amplitude = scaled.astype(jnp.bfloat16)
        mixed = (2.0 * scaled.T - scaled).astype(jnp.bfloat16)
        term = jnp.dot(amplitude, mixed, preferred_element_type=jnp.float32)
        total = term if total is None else total + term
    out_ref[...] = total


def add_pairs(density, turned, visitors, energies, column, row):
    nvir = turned.shape[0]
    whole = pl.BlockSpec(memory_space=pltpu.VMEM)
    operands = [energies, column, row, turned, *visitors]
    specs = [pl.BlockSpec(memory_space=pltpu.SMEM)] + [whole] * (len(operands) - 1)
    aliases = {}
    if density is not None:
        aliases = {len(operands): 0}
        operands.append(density)
        specs.append(whole)
    return pl.pallas_call(
        lambda *refs: pair_kernel(len(visitors), *refs),
        in_specs=specs,
        out_specs=whole,
        out_shape=jax.ShapeDtypeStruct((nvir, nvir), jnp.float32),
        input_output_aliases=aliases,
        compiler_params=pltpu.CompilerParams(vmem_limit_bytes=VMEM_LIMIT),
        name="pairs",
    )(*operands)


def shards(ints, occ_coef, vir_coef, occ_energy, vir_energy):
    aux_count, ao_count = lax.axis_size("aux"), lax.axis_size("ao")
    block, side = lax.axis_index("aux"), lax.axis_index("ao")
    parity = side ^ flipped(block)
    nvir = vir_coef.shape[1]

    slots = [0] * (aux_count * ao_count)
    for b in range(aux_count):
        for s in range(ao_count):
            slots[b * ao_count + (s ^ flipped(b))] = b * ao_count + s
    tiles = transform(ints, occ_coef, vir_coef, slots)
    arrived = lax.all_to_all(tiles, BOTH, split_axis=0, concat_axis=0, tiled=True)
    own, turned = combine(arrived.reshape(aux_count, ao_count, *arrived.shape[1:]))

    def shifted(value, distance):
        route = []
        for b in range(aux_count):
            source = (b - distance) % aux_count
            for s in range(ao_count):
                p = s ^ flipped(b)
                route.append((source * ao_count + (p ^ flipped(source)), b * ao_count + s))
        return lax.ppermute(value, BOTH, route)

    swap = [(0, 1), (1, 0)]
    below, above = shifted(own, 1), shifted(own, -1)
    turned_other = lax.ppermute(turned, "ao", swap)

    column, row = vir_energy[:, None], vir_energy[None, :]

    def occupied(b, p):
        return occ_energy[((b + aux_count) % aux_count) * ao_count + p]

    e_own, e_other = occupied(block, parity), occupied(block, 1 - parity)

    def energies(first, distances):
        return jnp.stack([first + occupied(block + d, parity) for d in distances])

    dens = add_pairs(None, turned, [own], energies(e_own, [0]), column, row)
    dens_other = None
    visitors, distances = [own], [0]
    for offset in range(1, CYCLE + 1):
        if offset > 1:
            visitors, distances = [], []
        pair, gaps = [below, above], [-offset, offset]
        if offset < CYCLE:
            below, above = shifted(below, 1), shifted(above, -1)
        dens = add_pairs(dens, turned, pair, energies(e_own, gaps), column, row)
        dens_other = add_pairs(
            dens_other,
            turned_other,
            visitors + pair,
            energies(e_other, distances + gaps),
            column,
            row,
        )

    half = nvir // ao_count

    def exchanged(kept, sent):
        sent = lax.dynamic_slice_in_dim(sent, (1 - side) * half, half).astype(jnp.bfloat16)
        kept = lax.dynamic_slice_in_dim(kept, side * half, half)
        return kept + lax.ppermute(sent, "ao", swap).astype(jnp.float32)

    results = [exchanged(dens, dens_other), exchanged(dens_other, dens)]
    low = jnp.where(parity == 0, results[0], results[1])
    high = jnp.where(parity == 0, results[1], results[0])
    return jnp.stack([low, high])


def solution(mesh):
    return jax.shard_map(
        shards,
        mesh=mesh,
        in_specs=(P("aux", "ao", None), P(), P("ao", None), P(), P()),
        out_specs=P("aux", "ao", None),
        check_vma=False,
    )
```

```python
import jax
import jax.numpy as jnp
from jax import lax
from jax.experimental import pallas as pl
from jax.experimental.pallas import tpu as pltpu
from jax.sharding import PartitionSpec as P

ROW = 8
LANES = 128
BOTH = ("aux", "ao")
MIB = 1024 * 1024
SWAP = [(0, 1), (1, 0)]


def flipped(block):
    return (block // ROW) % 2


def params(mib):
    return pltpu.CompilerParams(vmem_limit_bytes=mib * MIB)


def transform_kernel(slots, ints_ref, occ_ref, vir_ref, out_ref, held_ref):
    step = pl.program_id(0)
    chunk, rows, width = ints_ref.shape
    nocc, nvir = occ_ref.shape[1], vir_ref.shape[1]
    count = out_ref.shape[1]
    stride = nocc + 8
    slab = ints_ref[...].reshape(chunk * rows, width)
    half = jnp.dot(slab, occ_ref[...], preferred_element_type=jnp.float32)
    turned = [half[k * rows : (k + 1) * rows].T.astype(jnp.bfloat16) for k in range(chunk)]
    part = jnp.dot(
        jnp.concatenate(turned, axis=0), vir_ref[...], preferred_element_type=jnp.float32
    )
    for k in range(chunk):
        for column in range(nvir // LANES):
            start = pl.multiple_of((column * count + step * chunk + k) * stride, 8)
            held_ref[pl.ds(start, nocc), :] = part[
                k * nocc : (k + 1) * nocc, column * LANES : (column + 1) * LANES
            ]

    @pl.when(step == pl.num_programs(0) - 1)
    def _():
        for orbital in range(nocc):
            for column in range(nvir // LANES):
                tile = held_ref[pl.ds(column * count * stride + orbital, count, stride=stride), :]
                out_ref[slots[orbital], :, column * LANES : (column + 1) * LANES] = tile.astype(
                    jnp.bfloat16
                )


def transform(ints, occ_coef, vir_coef, slots, chunk=4):
    count, rows, width = ints.shape
    nocc, nvir = occ_coef.shape[1], vir_coef.shape[1]
    return pl.pallas_call(
        lambda *refs: transform_kernel(slots, *refs),
        grid=(count // chunk,),
        in_specs=[
            pl.BlockSpec((chunk, rows, width), lambda s: (s, 0, 0)),
            pl.BlockSpec((width, nocc), lambda s: (0, 0)),
            pl.BlockSpec((rows, nvir), lambda s: (0, 0)),
        ],
        out_specs=pl.BlockSpec((nocc, count, nvir), lambda s: (0, 0, 0)),
        out_shape=jax.ShapeDtypeStruct((nocc, count, nvir), jnp.bfloat16),
        scratch_shapes=[pltpu.VMEM((count * (nocc + 8) * nvir // LANES, LANES), jnp.float32)],
        compiler_params=params(56),
        name="transform",
    )(ints, occ_coef, vir_coef)


def combine_kernel(in_ref, energy_ref, own_ref, turned_ref, column_ref):
    tiles = in_ref[...].astype(jnp.float32)
    total = (tiles[:, 0] + tiles[:, 1]).reshape(own_ref.shape)
    own_ref[...] = total.astype(jnp.bfloat16)
    turned_ref[...] = total.T.astype(jnp.bfloat16)

    @pl.when(pl.program_id(0) == 0)
    def _():
        column_ref[...] = jnp.broadcast_to(energy_ref[...], (LANES, energy_ref.shape[1])).T


def combine(arrived, vir_energy, chunk=16):
    owners, halves, count, nvir = arrived.shape
    naux = owners * count
    return pl.pallas_call(
        combine_kernel,
        grid=(owners // chunk,),
        in_specs=[
            pl.BlockSpec((chunk, halves, count, nvir), lambda s: (s, 0, 0, 0)),
            pl.BlockSpec((1, nvir), lambda s: (0, 0)),
        ],
        out_specs=[
            pl.BlockSpec((chunk * count, nvir), lambda s: (s, 0)),
            pl.BlockSpec((nvir, chunk * count), lambda s: (0, s)),
            pl.BlockSpec((nvir, LANES), lambda s: (0, 0)),
        ],
        out_shape=[
            jax.ShapeDtypeStruct((naux, nvir), jnp.bfloat16),
            jax.ShapeDtypeStruct((nvir, naux), jnp.bfloat16),
            jax.ShapeDtypeStruct((nvir, LANES), jnp.float32),
        ],
        compiler_params=params(24),
        name="combine",
    )(arrived, vir_energy)


def pair_kernel(own_sides, distances, started, last, aux_count, *refs):
    refs = list(refs)
    energy_ref, column_ref, row_ref = refs[:3]
    turned_refs = refs[3 : 3 + len(own_sides)]
    visitor_refs = refs[3 + len(own_sides) :][: len(distances)]
    refs = refs[3 + len(own_sides) + len(distances) :]
    block, side = lax.axis_index("aux"), lax.axis_index("ao")
    parity = lax.rem(side + lax.rem(lax.div(block, ROW), 2), 2)
    odd = lax.rem(block, 2)
    nvir = row_ref.shape[1]
    column = column_ref[...]
    vir_pairs = jnp.concatenate([column] * (nvir // LANES), axis=1) + row_ref[...]
    for n, own_side in enumerate(own_sides):
        mine = parity if own_side == 0 else 1 - parity
        e_own = energy_ref[2 * block + mine]
        total = refs[n][...] if started else None
        for (even_distance, odd_distance), visitor_ref in zip(distances, visitor_refs):
            distance = even_distance + (odd_distance - even_distance) * odd
            visiting = lax.rem(block + distance + aux_count, aux_count)
            e_pair = e_own + energy_ref[2 * visiting + parity]
            integrals = jnp.dot(
                turned_refs[n][...], visitor_ref[...], preferred_element_type=jnp.float32
            )
            scaled = integrals / (e_pair - vir_pairs)
            amplitude = scaled.astype(jnp.bfloat16)
            mixed = (2.0 * scaled.T - scaled).astype(jnp.bfloat16)
            term = jnp.dot(amplitude, mixed, preferred_element_type=jnp.float32)
            total = term if total is None else total + term
        if not last:
            refs[len(own_sides) * started + n][...] = total
        else:
            kept_ref, sent_ref, held_ref = refs[1:]
            half = kept_ref.shape[0]
            held_ref[...] = total
            kept_ref[...] = held_ref[pl.ds(pl.multiple_of(side * half, half), half), :]
            sent_ref[...] = held_ref[
                pl.ds(pl.multiple_of((1 - side) * half, half), half), :
            ].astype(jnp.bfloat16)


def add_pairs(energies, turned, visitors, density, last=False):
    occ_energy, column, row = energies
    sides = sorted(turned)
    nvir, naux = turned[sides[0]].shape
    whole = pl.BlockSpec(memory_space=pltpu.VMEM)
    operands = [occ_energy, column, row]
    operands += [turned[s] for s in sides] + [v for _, v in visitors]
    specs = [pl.BlockSpec(memory_space=pltpu.SMEM)] + [whole] * (len(operands) - 1)
    started = density is not None
    aliases = {}
    square = jax.ShapeDtypeStruct((nvir, nvir), jnp.float32)
    if started:
        if not last:
            aliases = {len(operands) + n: n for n in range(len(sides))}
        operands += [density[s] for s in sides]
        specs += [whole] * len(sides)
    if last:
        out_shape = [
            jax.ShapeDtypeStruct((nvir // 2, nvir), jnp.float32),
            jax.ShapeDtypeStruct((nvir // 2, nvir), jnp.bfloat16),
        ]
        scratch = [pltpu.VMEM((nvir, nvir), jnp.float32)]
    else:
        out_shape = [square] * len(sides)
        scratch = []
    pairs = len(sides) * len(visitors)
    results = pl.pallas_call(
        lambda *refs: pair_kernel(
            sides, [d for d, _ in visitors], started, last, lax.axis_size("aux"), *refs
        ),
        in_specs=specs,
        out_specs=[whole] * len(out_shape),
        out_shape=out_shape,
        scratch_shapes=scratch,
        input_output_aliases=aliases,
        compiler_params=params(16),
        cost_estimate=pl.CostEstimate(
            flops=pairs * 2 * nvir * nvir * (naux + nvir),
            bytes_accessed=pairs * 2 * nvir * naux,
            transcendentals=0,
        ),
        name="pairs",
    )(*operands)
    return results if last else dict(zip(sides, results))


def finish_kernel(kept_own, came_own, kept_other, came_other, out_ref):
    block, side = lax.axis_index("aux"), lax.axis_index("ao")
    parity = lax.rem(side + lax.rem(lax.div(block, ROW), 2), 2)
    out_ref[parity] = kept_own[...] + came_own[...].astype(jnp.float32)
    out_ref[1 - parity] = kept_other[...] + came_other[...].astype(jnp.float32)


def finish(*operands):
    rows, nvir = operands[0].shape
    whole = pl.BlockSpec(memory_space=pltpu.VMEM)
    return pl.pallas_call(
        finish_kernel,
        in_specs=[whole] * 4,
        out_specs=whole,
        out_shape=jax.ShapeDtypeStruct((2, rows, nvir), jnp.float32),
        compiler_params=params(16),
        name="finish",
    )(*operands)


def shards(ints, occ_coef, vir_coef, occ_energy, vir_energy):
    aux_count, ao_count = lax.axis_size("aux"), lax.axis_size("ao")
    odd = lax.axis_index("aux") % 2

    def place(block, parity):
        return block * ao_count + (parity ^ flipped(block))

    every = [(b, p) for b in range(aux_count) for p in range(ao_count)]

    def shifted(value, distance):
        route = [(place((b - distance) % aux_count, p), place(b, p)) for b, p in every]
        return lax.ppermute(value, BOTH, route)

    def across(value):
        return lax.ppermute(value, "aux", [(b ^ 1, b) for b in range(aux_count)])

    def over(value):
        return lax.ppermute(value, "ao", SWAP)

    slots = [place(b, p) for b, p in every]
    tiles = transform(ints, occ_coef, vir_coef, slots)
    arrived = lax.all_to_all(tiles, BOTH, split_axis=0, concat_axis=0, tiled=True)
    row = vir_energy[None, :]
    own, turned, column = combine(arrived.reshape(aux_count, ao_count, *arrived.shape[1:]), row)
    energies = (occ_energy, column, row)

    hold = lax.optimization_barrier
    below, above = shifted(own, 2), shifted(own, -2)
    neighbour = across(own)
    turned_other = over(turned)
    first = [((0, 0), own), ((1, -1), neighbour)]
    density = add_pairs(energies, {0: turned}, first, None)
    turned_other, density = hold((turned_other, density))
    both = {0: turned, 1: turned_other}
    density |= add_pairs(energies, {1: turned_other}, first, None)
    below, above, density = hold((below, above, density))

    far_below, far_above = shifted(below, 2), shifted(above, -2)
    next_below, next_above = across(below), across(above)
    density = add_pairs(energies, both, [((-2, -2), below), ((2, 2), above)], density)
    next_below, next_above, density = hold((next_below, next_above, density))
    density = add_pairs(energies, both, [((-1, -3), next_below), ((3, 1), next_above)], density)
    far_below, far_above, density = hold((far_below, far_above, density))

    remaining = across(jnp.where(odd == 0, far_above, far_below))
    density = add_pairs(energies, both, [((-4, -4), far_below), ((4, 4), far_above)], density)
    remaining, density = hold((remaining, density))
    final = [((-3, 3), remaining)]
    kept_own, sent_own = add_pairs(energies, {0: turned}, final, {0: density[0]}, last=True)
    came_other = over(sent_own)
    kept_other, sent_other = add_pairs(
        energies, {1: turned_other}, final, {1: density[1]}, last=True
    )
    came_own = over(sent_other)
    return finish(kept_own, came_own, kept_other, came_other)


def solution(mesh):
    return jax.shard_map(
        shards,
        mesh=mesh,
        in_specs=(P("aux", "ao", None), P(), P("ao", None), P(), P()),
        out_specs=P("aux", "ao", None),
        check_vma=False,
    )
```

```python
import jax
import jax.numpy as jnp
from jax import lax
from jax.experimental import pallas as pl
from jax.experimental.pallas import tpu as pltpu
from jax.sharding import PartitionSpec as P

ROW = 8
LANES = 128
BOTH = ("aux", "ao")
MIB = 1024 * 1024
SWAP = [(0, 1), (1, 0)]


def flipped(block):
    return (block // ROW) % 2


def params(mib):
    return pltpu.CompilerParams(vmem_limit_bytes=mib * MIB)


def transform_kernel(slots, group, ints_ref, occ_ref, out_ref, held_ref):
    step = pl.program_id(0)
    chunk, rows, width = ints_ref.shape
    nocc = occ_ref.shape[1]
    stride = nocc + 8
    slab = ints_ref[...].reshape(chunk * rows, width)
    half = jnp.dot(slab, occ_ref[...], preferred_element_type=jnp.float32)
    for k in range(chunk):
        turned = half[k * rows : (k + 1) * rows].T
        for column in range(rows // LANES):
            start = (column * group + lax.rem(step * chunk, group) + k) * stride
            held_ref[pl.ds(pl.multiple_of(start, 8), nocc), :] = turned[
                :, column * LANES : (column + 1) * LANES
            ]

    @pl.when(lax.rem((step + 1) * chunk, group) == 0)
    def _():
        first = pl.multiple_of((step + 1) * chunk - group, group)
        for orbital in range(nocc):
            for column in range(rows // LANES):
                tile = held_ref[pl.ds(column * group * stride + orbital, group, stride=stride), :]
                out_ref[
                    slots[orbital], pl.ds(first, group), column * LANES : (column + 1) * LANES
                ] = tile.astype(jnp.bfloat16)


def transform(ints, occ_coef, slots, chunk=8, group=8):
    count, rows, width = ints.shape
    nocc = occ_coef.shape[1]
    return pl.pallas_call(
        lambda *refs: transform_kernel(slots, group, *refs),
        grid=(count // chunk,),
        in_specs=[
            pl.BlockSpec((chunk, rows, width), lambda s: (s, 0, 0)),
            pl.BlockSpec((width, nocc), lambda s: (0, 0)),
        ],
        out_specs=pl.BlockSpec((nocc, count, rows), lambda s: (0, 0, 0)),
        out_shape=jax.ShapeDtypeStruct((nocc, count, rows), jnp.bfloat16),
        scratch_shapes=[pltpu.VMEM((group * (nocc + 8) * rows // LANES, LANES), jnp.float32)],
        compiler_params=params(56),
        name="transform",
    )(ints, occ_coef)


def combine_kernel(in_ref, vir_ref, vir_other_ref, energy_ref, own_ref, turned_ref, column_ref):
    side = lax.axis_index("ao")
    owners, halves, count, rows = in_ref.shape
    mine = in_ref[:, side].reshape(owners * count, rows)
    others = in_ref[:, 1 - side].reshape(owners * count, rows)
    total = jnp.dot(mine, vir_ref[...], preferred_element_type=jnp.float32)
    total += jnp.dot(others, vir_other_ref[...], preferred_element_type=jnp.float32)
    own_ref[...] = total.astype(jnp.bfloat16)
    turned_ref[...] = total.T.astype(jnp.bfloat16)
    column_ref[...] = jnp.broadcast_to(energy_ref[...], (LANES, energy_ref.shape[1])).T


def combine(arrived, vir, vir_other, vir_energy):
    owners, halves, count, rows = arrived.shape
    naux, nvir = owners * count, vir.shape[1]
    whole = pl.BlockSpec(memory_space=pltpu.VMEM)
    return pl.pallas_call(
        combine_kernel,
        in_specs=[whole] * 4,
        out_specs=[whole] * 3,
        out_shape=[
            jax.ShapeDtypeStruct((naux, nvir), jnp.bfloat16),
            jax.ShapeDtypeStruct((nvir, naux), jnp.bfloat16),
            jax.ShapeDtypeStruct((nvir, LANES), jnp.float32),
        ],
        compiler_params=params(16),
        name="combine",
    )(arrived, vir, vir_other, vir_energy)


def pair_kernel(sides, plan, started, last, aux_count, *refs):
    energy_ref, column_ref, row_ref, *refs = refs
    turned_refs = dict(zip(sides, refs))
    refs = refs[len(sides) :]
    visitor_refs, refs = refs[: len(plan)], refs[len(plan) :]
    started_refs = dict(zip(started, refs))
    refs = refs[len(started) :]
    block, side = lax.axis_index("aux"), lax.axis_index("ao")
    parity = lax.rem(side + lax.rem(lax.div(block, ROW), 2), 2)
    odd = lax.rem(block, 2)
    nvir = row_ref.shape[1]
    vir_pairs = jnp.concatenate([column_ref[...]] * (nvir // LANES), axis=1) + row_ref[...]
    for n, own_side in enumerate(sides):
        mine = parity if own_side == 0 else 1 - parity
        e_own = energy_ref[2 * block + mine]
        total = started_refs[own_side][...] if own_side in started_refs else None
        for ((even_distance, odd_distance), wanted), visitor_ref in zip(plan, visitor_refs):
            if own_side not in wanted:
                continue
            distance = even_distance + (odd_distance - even_distance) * odd
            visiting = lax.rem(block + distance + aux_count, aux_count)
            e_pair = e_own + energy_ref[2 * visiting + parity]
            integrals = jnp.dot(
                turned_refs[own_side][...], visitor_ref[...], preferred_element_type=jnp.float32
            )
            scaled = integrals / (e_pair - vir_pairs)
            amplitude = scaled.astype(jnp.bfloat16)
            mixed = (2.0 * scaled.T - scaled).astype(jnp.bfloat16)
            term = jnp.dot(amplitude, mixed, preferred_element_type=jnp.float32)
            total = term if total is None else total + term
        if not last:
            refs[n][...] = total
        else:
            kept_ref, *sent_refs, held_ref = refs
            half = kept_ref.shape[0]
            held_ref[...] = total
            kept_ref[...] = held_ref[pl.ds(pl.multiple_of(side * half, half), half), :]
            start = (1 - side) * half
            for sent_ref in sent_refs:
                rows = sent_ref.shape[0]
                sent_ref[...] = held_ref[pl.ds(pl.multiple_of(start, rows), rows), :].astype(
                    jnp.bfloat16
                )
                start = start + rows


def add_pairs(energies, turned, visitors, density, last=0):
    sides, started = sorted(turned), sorted(density)
    nvir, naux = turned[sides[0]].shape
    plan = [(d, w) for d, _, w in visitors]
    operands = [*energies] + [turned[s] for s in sides] + [v for _, v, _ in visitors]
    aliases = {}
    if not last:
        aliases = {len(operands) + n: sides.index(s) for n, s in enumerate(started)}
    operands += [density[s] for s in started]
    whole = pl.BlockSpec(memory_space=pltpu.VMEM)
    specs = [pl.BlockSpec(memory_space=pltpu.SMEM)] + [whole] * (len(operands) - 1)
    if last:
        half = nvir // 2
        out_shape = [jax.ShapeDtypeStruct((half, nvir), jnp.float32)]
        out_shape += [jax.ShapeDtypeStruct((half // last, nvir), jnp.bfloat16)] * last
        scratch = [pltpu.VMEM((nvir, nvir), jnp.float32)]
    else:
        out_shape = [jax.ShapeDtypeStruct((nvir, nvir), jnp.float32)] * len(sides)
        scratch = []
    pairs = sum(len(w) for _, w in plan)
    results = pl.pallas_call(
        lambda *refs: pair_kernel(sides, plan, started, last, lax.axis_size("aux"), *refs),
        in_specs=specs,
        out_specs=[whole] * len(out_shape),
        out_shape=out_shape,
        scratch_shapes=scratch,
        input_output_aliases=aliases,
        compiler_params=params(16),
        cost_estimate=pl.CostEstimate(
            flops=pairs * 2 * nvir * nvir * (naux + nvir),
            bytes_accessed=pairs * 2 * nvir * naux,
            transcendentals=0,
        ),
        name="pairs",
    )(*operands)
    return results if last else dict(zip(sides, results))


def finish_kernel(kept_own, kept_other, *refs):
    *came_refs, out_ref = refs
    block, side = lax.axis_index("aux"), lax.axis_index("ao")
    parity = lax.rem(side + lax.rem(lax.div(block, ROW), 2), 2)
    out_ref[parity] = kept_own[...] + came_refs[0][...].astype(jnp.float32)
    start = 0
    for came_ref in came_refs[1:]:
        rows = came_ref.shape[0]
        out_ref[1 - parity, start : start + rows] = kept_other[
            start : start + rows
        ] + came_ref[...].astype(jnp.float32)
        start += rows


def finish(*operands):
    rows, nvir = operands[0].shape
    whole = pl.BlockSpec(memory_space=pltpu.VMEM)
    return pl.pallas_call(
        finish_kernel,
        in_specs=[whole] * len(operands),
        out_specs=whole,
        out_shape=jax.ShapeDtypeStruct((2, rows, nvir), jnp.float32),
        compiler_params=params(16),
        name="finish",
    )(*operands)


def shards(ints, occ_coef, vir_coef, occ_energy, vir_energy):
    aux_count, ao_count = lax.axis_size("aux"), lax.axis_size("ao")
    odd = lax.axis_index("aux") % 2

    def place(block, parity):
        return block * ao_count + (parity ^ flipped(block))

    every = [(b, p) for b in range(aux_count) for p in range(ao_count)]

    def shifted(value, distance):
        route = [(place((b - distance) % aux_count, p), place(b, p)) for b, p in every]
        return lax.ppermute(value, BOTH, route)

    def across(value):
        return lax.ppermute(value, "aux", [(b ^ 1, b) for b in range(aux_count)])

    def over(value):
        return lax.ppermute(value, "ao", SWAP)

    hold = lax.optimization_barrier
    slots = [place(b, p) for b, p in every]
    vir_other = over(vir_coef)
    tiles = transform(ints, occ_coef, slots)
    arrived = lax.all_to_all(tiles, BOTH, split_axis=0, concat_axis=0, tiled=True)
    arrived = arrived.reshape(aux_count, ao_count, *arrived.shape[1:])
    arrived, vir_other = hold((arrived, vir_other))
    row = vir_energy[None, :]
    own, turned, column = combine(arrived, vir_coef, vir_other, row)
    energies = (occ_energy, column, row)

    below, above = shifted(own, 2), shifted(own, -2)
    neighbour, turned_other = across(own), over(turned)
    own_pairs = [((0, 0), own), ((1, -1), neighbour)]
    mine = add_pairs(energies, {0: turned}, [(*v, (0,)) for v in own_pairs], {})
    below, above, mine = hold((below, above, mine))
    far_below, far_above = shifted(below, 2), shifted(above, -2)
    next_below, next_above = across(below), across(above)

    turned_other, mine = hold((turned_other, mine))
    both = {0: turned, 1: turned_other}
    near = [((-2, -2), below), ((2, 2), above), ((-1, -3), next_below), ((3, 1), next_above)]
    plan = [(*v, (1,)) for v in own_pairs] + [(*v, (0, 1)) for v in near]
    density = add_pairs(energies, both, plan, mine)
    far_below, far_above, density = hold((far_below, far_above, density))

    remaining = across(jnp.where(odd == 0, far_above, far_below))
    far = [((-4, -4), far_below), ((4, 4), far_above)]
    final = [((-3, 3), remaining)]
    other = add_pairs(energies, {1: turned_other}, [(*v, (1,)) for v in far], {1: density[1]})
    remaining, other = hold((remaining, other))
    kept_other, sent = add_pairs(
        energies, {1: turned_other}, [(*v, (1,)) for v in final], other, last=1
    )
    came_own = over(sent)
    turned, sent = hold((turned, sent))
    kept_own, *sent = add_pairs(
        energies, {0: turned}, [(*v, (0,)) for v in far + final], {0: density[0]}, last=2
    )
    return finish(kept_own, kept_other, came_own, *[over(piece) for piece in sent])


def solution(mesh):
    return jax.shard_map(
        shards,
        mesh=mesh,
        in_specs=(P("aux", "ao", None), P(), P("ao", None), P(), P()),
        out_specs=P("aux", "ao", None),
        check_vma=False,
    )
```

```python
import jax
import jax.numpy as jnp
from jax import lax
from jax.experimental import pallas as pl
from jax.experimental.pallas import tpu as pltpu
from jax.sharding import PartitionSpec as P

ROW = 8
LANES = 128
BOTH = ("aux", "ao")
MIB = 1024 * 1024
SWAP = [(0, 1), (1, 0)]


def flipped(block):
    return (block // ROW) % 2


def params(mib):
    return pltpu.CompilerParams(vmem_limit_bytes=mib * MIB)


def transform_kernel(slots, group, ints_ref, occ_ref, out_ref, held_ref):
    step = pl.program_id(0)
    chunk, rows, width = ints_ref.shape
    nocc = occ_ref.shape[1]
    stride = nocc + 8
    slab = ints_ref[...].reshape(chunk * rows, width)
    half = jnp.dot(slab, occ_ref[...], preferred_element_type=jnp.float32)
    for k in range(chunk):
        turned = half[k * rows : (k + 1) * rows].T
        for column in range(rows // LANES):
            start = (column * group + lax.rem(step * chunk, group) + k) * stride
            held_ref[pl.ds(pl.multiple_of(start, 8), nocc), :] = turned[
                :, column * LANES : (column + 1) * LANES
            ]

    @pl.when(lax.rem((step + 1) * chunk, group) == 0)
    def _():
        first = pl.multiple_of((step + 1) * chunk - group, group)
        for orbital in range(nocc):
            for column in range(rows // LANES):
                tile = held_ref[pl.ds(column * group * stride + orbital, group, stride=stride), :]
                out_ref[
                    slots[orbital], pl.ds(first, group), column * LANES : (column + 1) * LANES
                ] = tile.astype(jnp.bfloat16)


def transform(ints, occ_coef, slots, chunk=8, group=8):
    count, rows, width = ints.shape
    nocc = occ_coef.shape[1]
    return pl.pallas_call(
        lambda *refs: transform_kernel(slots, group, *refs),
        grid=(count // chunk,),
        in_specs=[
            pl.BlockSpec((chunk, rows, width), lambda s: (s, 0, 0)),
            pl.BlockSpec((width, nocc), lambda s: (0, 0)),
        ],
        out_specs=pl.BlockSpec((nocc, count, rows), lambda s: (0, 0, 0)),
        out_shape=jax.ShapeDtypeStruct((nocc, count, rows), jnp.bfloat16),
        scratch_shapes=[pltpu.VMEM((group * (nocc + 8) * rows // LANES, LANES), jnp.float32)],
        compiler_params=params(56),
        name="transform",
    )(ints, occ_coef)


def combine_kernel(in_ref, vir_ref, vir_other_ref, energy_ref, own_ref, turned_ref, column_ref):
    side = lax.axis_index("ao")
    owners, halves, count, rows = in_ref.shape
    mine = in_ref[:, side].reshape(owners * count, rows)
    others = in_ref[:, 1 - side].reshape(owners * count, rows)
    total = jnp.dot(mine, vir_ref[...], preferred_element_type=jnp.float32)
    total += jnp.dot(others, vir_other_ref[...], preferred_element_type=jnp.float32)
    own_ref[...] = total.astype(jnp.bfloat16)
    turned_ref[...] = total.T.astype(jnp.bfloat16)
    column_ref[...] = jnp.broadcast_to(energy_ref[...], (LANES, energy_ref.shape[1])).T


def combine(arrived, vir, vir_other, vir_energy):
    owners, halves, count, rows = arrived.shape
    naux, nvir = owners * count, vir.shape[1]
    whole = pl.BlockSpec(memory_space=pltpu.VMEM)
    return pl.pallas_call(
        combine_kernel,
        in_specs=[whole] * 4,
        out_specs=[whole] * 3,
        out_shape=[
            jax.ShapeDtypeStruct((naux, nvir), jnp.bfloat16),
            jax.ShapeDtypeStruct((nvir, naux), jnp.bfloat16),
            jax.ShapeDtypeStruct((nvir, LANES), jnp.float32),
        ],
        compiler_params=params(16),
        name="combine",
    )(arrived, vir, vir_other, vir_energy)


def pair_kernel(sides, plan, started, last, aux_count, *refs):
    energy_ref, column_ref, row_ref, *refs = refs
    turned_refs = dict(zip(sides, refs))
    refs = refs[len(sides) :]
    visitor_refs, refs = refs[: len(plan)], refs[len(plan) :]
    started_refs = dict(zip(started, refs))
    refs = refs[len(started) :]
    block, side = lax.axis_index("aux"), lax.axis_index("ao")
    parity = lax.rem(side + lax.rem(lax.div(block, ROW), 2), 2)
    odd = lax.rem(block, 2)
    nvir = row_ref.shape[1]
    vir_pairs = jnp.concatenate([column_ref[...]] * (nvir // LANES), axis=1) + row_ref[...]
    jobs = []
    for own_side in sides:
        mine = parity if own_side == 0 else 1 - parity
        e_own = energy_ref[2 * block + mine]
        for ((even_distance, odd_distance), wanted), visitor_ref in zip(plan, visitor_refs):
            if own_side in wanted:
                distance = even_distance + (odd_distance - even_distance) * odd
                visiting = lax.rem(block + distance + aux_count, aux_count)
                e_pair = e_own + energy_ref[2 * visiting + parity]
                jobs.append((own_side, e_pair, visitor_ref))

    def integrals_of(own_side, e_pair, visitor_ref):
        return jnp.dot(
            turned_refs[own_side][...], visitor_ref[...], preferred_element_type=jnp.float32
        )

    totals = {s: started_refs[s][...] if s in started_refs else None for s in sides}
    upcoming = integrals_of(*jobs[0])
    for k, (own_side, e_pair, _) in enumerate(jobs):
        integrals = upcoming
        if k + 1 < len(jobs):
            upcoming = integrals_of(*jobs[k + 1])
        scaled = integrals / (e_pair - vir_pairs)
        amplitude = scaled.astype(jnp.bfloat16)
        mixed = (2.0 * scaled.T - scaled).astype(jnp.bfloat16)
        term = jnp.dot(amplitude, mixed, preferred_element_type=jnp.float32)
        totals[own_side] = term if totals[own_side] is None else totals[own_side] + term
    for n, own_side in enumerate(sides):
        total = totals[own_side]
        if not last:
            refs[n][...] = total
        else:
            kept_ref, *sent_refs, held_ref = refs
            half = kept_ref.shape[0]
            held_ref[...] = total
            kept_ref[...] = held_ref[pl.ds(pl.multiple_of(side * half, half), half), :]
            start = (1 - side) * half
            for sent_ref in sent_refs:
                rows = sent_ref.shape[0]
                sent_ref[...] = held_ref[pl.ds(pl.multiple_of(start, rows), rows), :].astype(
                    jnp.bfloat16
                )
                start = start + rows


def add_pairs(energies, turned, visitors, density, last=0):
    sides, started = sorted(turned), sorted(density)
    nvir, naux = turned[sides[0]].shape
    plan = [(d, w) for d, _, w in visitors]
    operands = [*energies] + [turned[s] for s in sides] + [v for _, v, _ in visitors]
    aliases = {}
    if not last:
        aliases = {len(operands) + n: sides.index(s) for n, s in enumerate(started)}
    operands += [density[s] for s in started]
    whole = pl.BlockSpec(memory_space=pltpu.VMEM)
    specs = [pl.BlockSpec(memory_space=pltpu.SMEM)] + [whole] * (len(operands) - 1)
    if last:
        half = nvir // 2
        out_shape = [jax.ShapeDtypeStruct((half, nvir), jnp.float32)]
        out_shape += [jax.ShapeDtypeStruct((half // last, nvir), jnp.bfloat16)] * last
        scratch = [pltpu.VMEM((nvir, nvir), jnp.float32)]
    else:
        out_shape = [jax.ShapeDtypeStruct((nvir, nvir), jnp.float32)] * len(sides)
        scratch = []
    pairs = sum(len(w) for _, w in plan)
    results = pl.pallas_call(
        lambda *refs: pair_kernel(sides, plan, started, last, lax.axis_size("aux"), *refs),
        in_specs=specs,
        out_specs=[whole] * len(out_shape),
        out_shape=out_shape,
        scratch_shapes=scratch,
        input_output_aliases=aliases,
        compiler_params=params(16),
        cost_estimate=pl.CostEstimate(
            flops=pairs * 2 * nvir * nvir * (naux + nvir),
            bytes_accessed=pairs * 2 * nvir * naux,
            transcendentals=0,
        ),
        name="pairs",
    )(*operands)
    return results if last else dict(zip(sides, results))


def finish_kernel(kept_own, kept_other, *refs):
    *came_refs, out_ref = refs
    block, side = lax.axis_index("aux"), lax.axis_index("ao")
    parity = lax.rem(side + lax.rem(lax.div(block, ROW), 2), 2)
    out_ref[parity] = kept_own[...] + came_refs[0][...].astype(jnp.float32)
    start = 0
    for came_ref in came_refs[1:]:
        rows = came_ref.shape[0]
        out_ref[1 - parity, start : start + rows] = kept_other[
            start : start + rows
        ] + came_ref[...].astype(jnp.float32)
        start += rows


def finish(*operands):
    rows, nvir = operands[0].shape
    whole = pl.BlockSpec(memory_space=pltpu.VMEM)
    return pl.pallas_call(
        finish_kernel,
        in_specs=[whole] * len(operands),
        out_specs=whole,
        out_shape=jax.ShapeDtypeStruct((2, rows, nvir), jnp.float32),
        compiler_params=params(16),
        name="finish",
    )(*operands)


def shards(ints, occ_coef, vir_coef, occ_energy, vir_energy):
    aux_count, ao_count = lax.axis_size("aux"), lax.axis_size("ao")
    odd = lax.axis_index("aux") % 2

    def place(block, parity):
        return block * ao_count + (parity ^ flipped(block))

    every = [(b, p) for b in range(aux_count) for p in range(ao_count)]

    def shifted(value, distance):
        route = [(place((b - distance) % aux_count, p), place(b, p)) for b, p in every]
        return lax.ppermute(value, BOTH, route)

    def across(value):
        return lax.ppermute(value, "aux", [(b ^ 1, b) for b in range(aux_count)])

    def over(value):
        return lax.ppermute(value, "ao", SWAP)

    hold = lax.optimization_barrier
    slots = [place(b, p) for b, p in every]
    vir_other = over(vir_coef)
    tiles = transform(ints, occ_coef, slots)
    arrived = lax.all_to_all(tiles, BOTH, split_axis=0, concat_axis=0, tiled=True)
    arrived = arrived.reshape(aux_count, ao_count, *arrived.shape[1:])
    arrived, vir_other = hold((arrived, vir_other))
    row = vir_energy[None, :]
    own, turned, column = combine(arrived, vir_coef, vir_other, row)
    energies = (occ_energy, column, row)

    below, above = shifted(own, 2), shifted(own, -2)
    neighbour, turned_other = across(own), over(turned)
    own_pairs = [((0, 0), own), ((1, -1), neighbour)]
    mine = add_pairs(energies, {0: turned}, [(*v, (0,)) for v in own_pairs], {})
    below, above, mine = hold((below, above, mine))
    far_below, far_above = shifted(below, 2), shifted(above, -2)
    next_below, next_above = across(below), across(above)

    turned_other, mine = hold((turned_other, mine))
    both = {0: turned, 1: turned_other}
    near = [((-2, -2), below), ((2, 2), above), ((-1, -3), next_below), ((3, 1), next_above)]
    plan = [(*v, (1,)) for v in own_pairs] + [(*v, (0, 1)) for v in near]
    density = add_pairs(energies, both, plan, mine)
    far_below, far_above, density = hold((far_below, far_above, density))

    remaining = across(jnp.where(odd == 0, far_above, far_below))
    far = [((-4, -4), far_below), ((4, 4), far_above)]
    final = [((-3, 3), remaining)]
    other = add_pairs(energies, {1: turned_other}, [(*v, (1,)) for v in far], {1: density[1]})
    remaining, other = hold((remaining, other))
    kept_other, sent = add_pairs(
        energies, {1: turned_other}, [(*v, (1,)) for v in final], other, last=1
    )
    came_own = over(sent)
    turned, sent = hold((turned, sent))
    kept_own, *sent = add_pairs(
        energies, {0: turned}, [(*v, (0,)) for v in far + final], {0: density[0]}, last=2
    )
    return finish(kept_own, kept_other, came_own, *[over(piece) for piece in sent])


def solution(mesh):
    return jax.shard_map(
        shards,
        mesh=mesh,
        in_specs=(P("aux", "ao", None), P(), P("ao", None), P(), P()),
        out_specs=P("aux", "ao", None),
        check_vma=False,
    )
```

```python
import jax
import jax.numpy as jnp
from jax import lax
from jax.experimental import pallas as pl
from jax.experimental.pallas import tpu as pltpu
from jax.sharding import PartitionSpec as P

ROW = 8
LANES = 128
BOTH = ("aux", "ao")
MIB = 1024 * 1024
SWAP = [(0, 1), (1, 0)]


def flipped(block):
    return (block // ROW) % 2


def params(mib):
    return pltpu.CompilerParams(vmem_limit_bytes=mib * MIB)


def transform_kernel(slots, group, ints_ref, occ_ref, out_ref, held_ref):
    step = pl.program_id(0)
    chunk, rows, width = ints_ref.shape
    nocc = occ_ref.shape[1]
    stride = nocc + 8
    slab = ints_ref[...].reshape(chunk * rows, width)
    half = jnp.dot(slab, occ_ref[...], preferred_element_type=jnp.float32)
    for k in range(chunk):
        turned = half[k * rows : (k + 1) * rows].T
        for column in range(rows // LANES):
            start = (column * group + lax.rem(step * chunk, group) + k) * stride
            held_ref[pl.ds(pl.multiple_of(start, 8), nocc), :] = turned[
                :, column * LANES : (column + 1) * LANES
            ]

    @pl.when(lax.rem((step + 1) * chunk, group) == 0)
    def _():
        first = pl.multiple_of((step + 1) * chunk - group, group)
        for orbital in range(nocc):
            for column in range(rows // LANES):
                tile = held_ref[pl.ds(column * group * stride + orbital, group, stride=stride), :]
                out_ref[
                    slots[orbital], pl.ds(first, group), column * LANES : (column + 1) * LANES
                ] = tile.astype(jnp.bfloat16)


def transform(ints, occ_coef, slots, chunk=8, group=8):
    count, rows, width = ints.shape
    nocc = occ_coef.shape[1]
    return pl.pallas_call(
        lambda *refs: transform_kernel(slots, group, *refs),
        grid=(count // chunk,),
        in_specs=[
            pl.BlockSpec((chunk, rows, width), lambda s: (s, 0, 0)),
            pl.BlockSpec((width, nocc), lambda s: (0, 0)),
        ],
        out_specs=pl.BlockSpec((nocc, count, rows), lambda s: (0, 0, 0)),
        out_shape=jax.ShapeDtypeStruct((nocc, count, rows), jnp.bfloat16),
        scratch_shapes=[pltpu.VMEM((group * (nocc + 8) * rows // LANES, LANES), jnp.float32)],
        compiler_params=params(56),
        name="transform",
    )(ints, occ_coef)


def combine_kernel(in_ref, vir_ref, vir_other_ref, energy_ref, own_ref, column_ref):
    side = lax.axis_index("ao")
    owners, halves, count, rows = in_ref.shape
    mine = in_ref[:, side].reshape(owners * count, rows)
    others = in_ref[:, 1 - side].reshape(owners * count, rows)
    total = jnp.dot(mine, vir_ref[...], preferred_element_type=jnp.float32)
    total += jnp.dot(others, vir_other_ref[...], preferred_element_type=jnp.float32)
    own_ref[...] = total.astype(jnp.bfloat16)
    column_ref[...] = jnp.broadcast_to(energy_ref[...], (LANES, energy_ref.shape[1])).T


def combine(arrived, vir, vir_other, vir_energy):
    owners, halves, count, rows = arrived.shape
    naux, nvir = owners * count, vir.shape[1]
    whole = pl.BlockSpec(memory_space=pltpu.VMEM)
    return pl.pallas_call(
        combine_kernel,
        in_specs=[whole] * 4,
        out_specs=[whole] * 2,
        out_shape=[
            jax.ShapeDtypeStruct((naux, nvir), jnp.bfloat16),
            jax.ShapeDtypeStruct((nvir, LANES), jnp.float32),
        ],
        compiler_params=params(16),
        name="combine",
    )(arrived, vir, vir_other, vir_energy)


def pair_kernel(sides, plan, started, last, turn, aux_count, *refs):
    energy_ref, column_ref, row_ref, *refs = refs
    turned_refs = {}
    if not turn:
        turned_refs = dict(zip(sides, refs))
        refs = refs[len(sides) :]
    visitor_refs, refs = refs[: len(plan)], refs[len(plan) :]
    if turn:
        turned_refs = {sides[0]: refs[-1]}
        refs[-1][...] = visitor_refs[0][...].T
    started_refs = dict(zip(started, refs))
    refs = refs[len(started) :]
    block, side = lax.axis_index("aux"), lax.axis_index("ao")
    parity = lax.rem(side + lax.rem(lax.div(block, ROW), 2), 2)
    odd = lax.rem(block, 2)
    nvir = row_ref.shape[1]
    vir_pairs = jnp.concatenate([column_ref[...]] * (nvir // LANES), axis=1) + row_ref[...]
    jobs = []
    for own_side in sides:
        mine = parity if own_side == 0 else 1 - parity
        e_own = energy_ref[2 * block + mine]
        for ((even_distance, odd_distance), wanted), visitor_ref in zip(plan, visitor_refs):
            if own_side in wanted:
                distance = even_distance + (odd_distance - even_distance) * odd
                visiting = lax.rem(block + distance + aux_count, aux_count)
                e_pair = e_own + energy_ref[2 * visiting + parity]
                jobs.append((own_side, e_pair, visitor_ref))

    def integrals_of(own_side, e_pair, visitor_ref):
        return jnp.dot(
            turned_refs[own_side][...], visitor_ref[...], preferred_element_type=jnp.float32
        )

    totals = {s: started_refs[s][...] if s in started_refs else None for s in sides}
    upcoming = integrals_of(*jobs[0])
    for k, (own_side, e_pair, _) in enumerate(jobs):
        integrals = upcoming
        if k + 1 < len(jobs):
            upcoming = integrals_of(*jobs[k + 1])
        scaled = integrals / (e_pair - vir_pairs)
        amplitude = scaled.astype(jnp.bfloat16)
        mixed = (2.0 * scaled.T - scaled).astype(jnp.bfloat16)
        term = jnp.dot(amplitude, mixed, preferred_element_type=jnp.float32)
        totals[own_side] = term if totals[own_side] is None else totals[own_side] + term
    for n, own_side in enumerate(sides):
        total = totals[own_side]
        if not last:
            refs[n][...] = total
        else:
            kept_ref, *sent_refs, held_ref = refs
            half = kept_ref.shape[0]
            held_ref[...] = total
            kept_ref[...] = held_ref[pl.ds(pl.multiple_of(side * half, half), half), :]
            start = (1 - side) * half
            for sent_ref in sent_refs:
                rows = sent_ref.shape[0]
                sent_ref[...] = held_ref[pl.ds(pl.multiple_of(start, rows), rows), :].astype(
                    jnp.bfloat16
                )
                start = start + rows


def add_pairs(energies, turned, visitors, density, last=0, turn=False):
    sides, started = [0] if turn else sorted(turned), sorted(density)
    naux, nvir = visitors[0][1].shape
    plan = [(d, w) for d, _, w in visitors]
    operands = [*energies] + ([] if turn else [turned[s] for s in sides]) + [v for _, v, _ in visitors]
    aliases = {}
    if not last:
        aliases = {len(operands) + n: sides.index(s) for n, s in enumerate(started)}
    operands += [density[s] for s in started]
    whole = pl.BlockSpec(memory_space=pltpu.VMEM)
    specs = [pl.BlockSpec(memory_space=pltpu.SMEM)] + [whole] * (len(operands) - 1)
    if last:
        half = nvir // 2
        out_shape = [jax.ShapeDtypeStruct((half, nvir), jnp.float32)]
        out_shape += [jax.ShapeDtypeStruct((half // last, nvir), jnp.bfloat16)] * last
        scratch = [pltpu.VMEM((nvir, nvir), jnp.float32)]
    else:
        out_shape = [jax.ShapeDtypeStruct((nvir, nvir), jnp.float32)] * len(sides)
        out_shape += [jax.ShapeDtypeStruct((nvir, naux), jnp.bfloat16)] * turn
        scratch = []
    pairs = sum(len(w) for _, w in plan)
    results = pl.pallas_call(
        lambda *refs: pair_kernel(sides, plan, started, last, turn, lax.axis_size("aux"), *refs),
        in_specs=specs,
        out_specs=[whole] * len(out_shape),
        out_shape=out_shape,
        scratch_shapes=scratch,
        input_output_aliases=aliases,
        compiler_params=params(16),
        cost_estimate=pl.CostEstimate(
            flops=pairs * 2 * nvir * nvir * (naux + nvir),
            bytes_accessed=pairs * 2 * nvir * naux,
            transcendentals=0,
        ),
        name="pairs",
    )(*operands)
    return results if last or turn else dict(zip(sides, results))


def finish_kernel(other, kept_ref, *refs):
    came_refs, (out_ref, held_ref, semaphore) = refs[: len(refs) - 3 - other], refs[-3:]
    block, side = lax.axis_index("aux"), lax.axis_index("ao")
    parity = lax.rem(side + lax.rem(lax.div(block, ROW), 2), 2)
    start = 0
    for came_ref in came_refs:
        rows = came_ref.shape[0]
        here = slice(start, start + rows)
        held_ref[here] = kept_ref[here] + came_ref[...].astype(jnp.float32)
        start += rows
    target = out_ref.at[1 - parity if other else parity]
    copy = pltpu.make_async_copy(held_ref, target, semaphore)
    copy.start()
    copy.wait()


def finish(other, kept, came, output):
    rows, nvir = kept.shape
    whole, anywhere = pl.BlockSpec(memory_space=pltpu.VMEM), pl.BlockSpec(memory_space=pl.ANY)
    operands, specs = [kept, *came], [whole] * (1 + len(came))
    if other:
        operands, specs = operands + [output], specs + [anywhere]
    return pl.pallas_call(
        lambda *refs: finish_kernel(other, *refs),
        in_specs=specs,
        out_specs=anywhere,
        out_shape=jax.ShapeDtypeStruct((2, rows, nvir), jnp.float32),
        scratch_shapes=[pltpu.VMEM((rows, nvir), jnp.float32), pltpu.SemaphoreType.DMA],
        input_output_aliases={len(operands) - 1: 0} if other else {},
        compiler_params=params(16),
        name="finish",
    )(*operands)


def shards(ints, occ_coef, vir_coef, occ_energy, vir_energy):
    aux_count, ao_count = lax.axis_size("aux"), lax.axis_size("ao")
    odd = lax.axis_index("aux") % 2

    def place(block, parity):
        return block * ao_count + (parity ^ flipped(block))

    every = [(b, p) for b in range(aux_count) for p in range(ao_count)]

    def shifted(value, distance):
        route = [(place((b - distance) % aux_count, p), place(b, p)) for b, p in every]
        return lax.ppermute(value, BOTH, route)

    def across(value):
        return lax.ppermute(value, "aux", [(b ^ 1, b) for b in range(aux_count)])

    def over(value):
        return lax.ppermute(value, "ao", SWAP)

    hold = lax.optimization_barrier
    slots = [place(b, p) for b, p in every]
    vir_other = over(vir_coef)
    tiles = transform(ints, occ_coef, slots)
    arrived = lax.all_to_all(tiles, BOTH, split_axis=0, concat_axis=0, tiled=True)
    arrived = arrived.reshape(aux_count, ao_count, *arrived.shape[1:])
    arrived, vir_other = hold((arrived, vir_other))
    row = vir_energy[None, :]
    own, column = combine(arrived, vir_coef, vir_other, row)
    energies = (occ_energy, column, row)

    below, above = shifted(own, 2), shifted(own, -2)
    neighbour = across(own)
    own_pairs = [((0, 0), own), ((1, -1), neighbour)]
    mine, turned = add_pairs(energies, {}, [(*v, (0,)) for v in own_pairs], {}, turn=True)
    mine, turned_other = {0: mine}, over(turned)
    below, above, mine = hold((below, above, mine))
    far_below, far_above = shifted(below, 2), shifted(above, -2)
    next_below, next_above = across(below), across(above)

    turned_other, mine = hold((turned_other, mine))
    both = {0: turned, 1: turned_other}
    near = [((-2, -2), below), ((2, 2), above), ((-1, -3), next_below), ((3, 1), next_above)]
    plan = [(*v, (1,)) for v in own_pairs] + [(*v, (0, 1)) for v in near]
    density = add_pairs(energies, both, plan, mine)
    far_below, far_above, density = hold((far_below, far_above, density))

    remaining = across(jnp.where(odd == 0, far_above, far_below))
    far = [((-4, -4), far_below), ((4, 4), far_above)]
    final = [((-3, 3), remaining)]
    other = add_pairs(energies, {1: turned_other}, [(*v, (1,)) for v in far], {1: density[1]})
    remaining, other = hold((remaining, other))
    kept_other, sent = add_pairs(
        energies, {1: turned_other}, [(*v, (1,)) for v in final], other, last=1
    )
    came_own = over(sent)
    turned, sent = hold((turned, sent))
    kept_own, *sent = add_pairs(
        energies, {0: turned}, [(*v, (0,)) for v in far + final], {0: density[0]}, last=2
    )
    came_other = [over(piece) for piece in sent]
    output = finish(0, kept_own, [came_own], None)
    came_other, output = hold((came_other, output))
    return finish(1, kept_other, came_other, output)


def solution(mesh):
    return jax.shard_map(
        shards,
        mesh=mesh,
        in_specs=(P("aux", "ao", None), P(), P("ao", None), P(), P()),
        out_specs=P("aux", "ao", None),
        check_vma=False,
    )
```

```python
import jax
import jax.numpy as jnp
from jax import lax
from jax.experimental import pallas as pl
from jax.experimental.pallas import tpu as pltpu
from jax.sharding import PartitionSpec as P

ROW = 8
LANES = 128
BOTH = ("aux", "ao")
MIB = 1024 * 1024
SWAP = [(0, 1), (1, 0)]


def flipped(block):
    return (block // ROW) % 2


def params(mib):
    return pltpu.CompilerParams(vmem_limit_bytes=mib * MIB)


def transform_kernel(slots, group, ints_ref, occ_ref, out_ref, held_ref):
    step = pl.program_id(0)
    chunk, rows, width = ints_ref.shape
    nocc = occ_ref.shape[1]
    stride = nocc + 8
    slab = ints_ref[...].reshape(chunk * rows, width)
    half = jnp.dot(slab, occ_ref[...], preferred_element_type=jnp.float32)
    for k in range(chunk):
        turned = half[k * rows : (k + 1) * rows].T
        for column in range(rows // LANES):
            start = (column * group + lax.rem(step * chunk, group) + k) * stride
            held_ref[pl.ds(pl.multiple_of(start, 8), nocc), :] = turned[
                :, column * LANES : (column + 1) * LANES
            ]

    @pl.when(lax.rem((step + 1) * chunk, group) == 0)
    def _():
        first = pl.multiple_of((step + 1) * chunk - group, group)
        for orbital in range(nocc):
            for column in range(rows // LANES):
                tile = held_ref[pl.ds(column * group * stride + orbital, group, stride=stride), :]
                out_ref[
                    slots[orbital], pl.ds(first, group), column * LANES : (column + 1) * LANES
                ] = tile.astype(jnp.bfloat16)


def transform(ints, occ_coef, slots, chunk=8, group=8):
    count, rows, width = ints.shape
    nocc = occ_coef.shape[1]
    return pl.pallas_call(
        lambda *refs: transform_kernel(slots, group, *refs),
        grid=(count // chunk,),
        in_specs=[
            pl.BlockSpec((chunk, rows, width), lambda s: (s, 0, 0)),
            pl.BlockSpec((width, nocc), lambda s: (0, 0)),
        ],
        out_specs=pl.BlockSpec((nocc, count, rows), lambda s: (0, 0, 0)),
        out_shape=jax.ShapeDtypeStruct((nocc, count, rows), jnp.bfloat16),
        scratch_shapes=[pltpu.VMEM((group * (nocc + 8) * rows // LANES, LANES), jnp.float32)],
        compiler_params=params(56),
        name="transform",
    )(ints, occ_coef)


def combine_kernel(in_ref, vir_ref, vir_other_ref, energy_ref, own_ref, column_ref):
    side = lax.axis_index("ao")
    owners, halves, count, rows = in_ref.shape
    mine = in_ref[:, side].reshape(owners * count, rows)
    others = in_ref[:, 1 - side].reshape(owners * count, rows)
    total = jnp.dot(mine, vir_ref[...], preferred_element_type=jnp.float32)
    total += jnp.dot(others, vir_other_ref[...], preferred_element_type=jnp.float32)
    own_ref[...] = total.astype(jnp.bfloat16)
    column_ref[...] = jnp.broadcast_to(energy_ref[...], (LANES, energy_ref.shape[1])).T


def combine(arrived, vir, vir_other, vir_energy):
    owners, halves, count, rows = arrived.shape
    naux, nvir = owners * count, vir.shape[1]
    whole = pl.BlockSpec(memory_space=pltpu.VMEM)
    return pl.pallas_call(
        combine_kernel,
        in_specs=[whole] * 4,
        out_specs=[whole] * 2,
        out_shape=[
            jax.ShapeDtypeStruct((naux, nvir), jnp.bfloat16),
            jax.ShapeDtypeStruct((nvir, LANES), jnp.float32),
        ],
        compiler_params=params(16),
        name="combine",
    )(arrived, vir, vir_other, vir_energy)


def pair_kernel(sides, plan, started, last, turn, aux_count, *refs):
    energy_ref, column_ref, row_ref, *refs = refs
    turned_refs = {}
    if not turn:
        turned_refs = dict(zip(sides, refs))
        refs = refs[len(sides) :]
    visitor_refs, refs = refs[: len(plan)], refs[len(plan) :]
    if turn:
        turned_refs = {sides[0]: refs[-1]}
        refs[-1][...] = visitor_refs[0][...].T
    started_refs = dict(zip(started, refs))
    refs = refs[len(started) :]
    block, side = lax.axis_index("aux"), lax.axis_index("ao")
    parity = lax.rem(side + lax.rem(lax.div(block, ROW), 2), 2)
    odd = lax.rem(block, 2)
    nvir = row_ref.shape[1]
    vir_pairs = jnp.concatenate([column_ref[...]] * (nvir // LANES), axis=1) + row_ref[...]
    jobs = []
    for own_side in sides:
        mine = parity if own_side == 0 else 1 - parity
        e_own = energy_ref[2 * block + mine]
        for ((even_distance, odd_distance), wanted), visitor_ref in zip(plan, visitor_refs):
            if own_side in wanted:
                distance = even_distance + (odd_distance - even_distance) * odd
                visiting = lax.rem(block + distance + aux_count, aux_count)
                e_pair = e_own + energy_ref[2 * visiting + parity]
                jobs.append((own_side, e_pair, visitor_ref))

    def integrals_of(own_side, e_pair, visitor_ref):
        return jnp.dot(
            turned_refs[own_side][...], visitor_ref[...], preferred_element_type=jnp.float32
        )

    totals = {s: started_refs[s][...] if s in started_refs else None for s in sides}
    upcoming = integrals_of(*jobs[0])
    for k, (own_side, e_pair, _) in enumerate(jobs):
        integrals = upcoming
        if k + 1 < len(jobs):
            upcoming = integrals_of(*jobs[k + 1])
        scaled = integrals / (e_pair - vir_pairs)
        amplitude = scaled.astype(jnp.bfloat16)
        mixed = (2.0 * scaled.T - scaled).astype(jnp.bfloat16)
        term = jnp.dot(amplitude, mixed, preferred_element_type=jnp.float32)
        totals[own_side] = term if totals[own_side] is None else totals[own_side] + term
    for n, own_side in enumerate(sides):
        total = totals[own_side]
        if not last:
            refs[n][...] = total
        else:
            kept_ref, *sent_refs, held_ref = refs
            half = kept_ref.shape[0]
            held_ref[...] = total
            kept_ref[...] = held_ref[pl.ds(pl.multiple_of(side * half, half), half), :]
            start = (1 - side) * half
            for sent_ref in sent_refs:
                rows = sent_ref.shape[0]
                sent_ref[...] = held_ref[pl.ds(pl.multiple_of(start, rows), rows), :].astype(
                    jnp.bfloat16
                )
                start = start + rows


def add_pairs(energies, turned, visitors, density, last=0, turn=False):
    sides, started = [0] if turn else sorted(turned), sorted(density)
    naux, nvir = visitors[0][1].shape
    plan = [(d, w) for d, _, w in visitors]
    operands = [*energies] + ([] if turn else [turned[s] for s in sides]) + [v for _, v, _ in visitors]
    aliases = {}
    if not last:
        aliases = {len(operands) + n: sides.index(s) for n, s in enumerate(started)}
    operands += [density[s] for s in started]
    whole = pl.BlockSpec(memory_space=pltpu.VMEM)
    specs = [pl.BlockSpec(memory_space=pltpu.SMEM)] + [whole] * (len(operands) - 1)
    if last:
        half = nvir // 2
        out_shape = [jax.ShapeDtypeStruct((half, nvir), jnp.float32)]
        out_shape += [jax.ShapeDtypeStruct((half // last, nvir), jnp.bfloat16)] * last
        scratch = [pltpu.VMEM((nvir, nvir), jnp.float32)]
    else:
        out_shape = [jax.ShapeDtypeStruct((nvir, nvir), jnp.float32)] * len(sides)
        out_shape += [jax.ShapeDtypeStruct((nvir, naux), jnp.bfloat16)] * turn
        scratch = []
    pairs = sum(len(w) for _, w in plan)
    results = pl.pallas_call(
        lambda *refs: pair_kernel(sides, plan, started, last, turn, lax.axis_size("aux"), *refs),
        in_specs=specs,
        out_specs=[whole] * len(out_shape),
        out_shape=out_shape,
        scratch_shapes=scratch,
        input_output_aliases=aliases,
        compiler_params=params(16),
        cost_estimate=pl.CostEstimate(
            flops=pairs * 2 * nvir * nvir * (naux + nvir),
            bytes_accessed=pairs * 2 * nvir * naux,
            transcendentals=0,
        ),
        name="pairs",
    )(*operands)
    return results if last or turn else dict(zip(sides, results))


def finish_kernel(other, kept_ref, *refs):
    came_refs, (out_ref, held_ref, semaphore) = refs[: len(refs) - 3 - other], refs[-3:]
    block, side = lax.axis_index("aux"), lax.axis_index("ao")
    parity = lax.rem(side + lax.rem(lax.div(block, ROW), 2), 2)
    start = 0
    for came_ref in came_refs:
        rows = came_ref.shape[0]
        here = slice(start, start + rows)
        held_ref[here] = kept_ref[here] + came_ref[...].astype(jnp.float32)
        start += rows
    target = out_ref.at[1 - parity if other else parity]
    copy = pltpu.make_async_copy(held_ref, target, semaphore)
    copy.start()
    copy.wait()


def finish(other, kept, came, output):
    rows, nvir = kept.shape
    whole, anywhere = pl.BlockSpec(memory_space=pltpu.VMEM), pl.BlockSpec(memory_space=pl.ANY)
    operands, specs = [kept, *came], [whole] * (1 + len(came))
    if other:
        operands, specs = operands + [output], specs + [anywhere]
    return pl.pallas_call(
        lambda *refs: finish_kernel(other, *refs),
        in_specs=specs,
        out_specs=anywhere,
        out_shape=jax.ShapeDtypeStruct((2, rows, nvir), jnp.float32),
        scratch_shapes=[pltpu.VMEM((rows, nvir), jnp.float32), pltpu.SemaphoreType.DMA],
        input_output_aliases={len(operands) - 1: 0} if other else {},
        compiler_params=params(16),
        name="finish",
    )(*operands)


def shards(ints, occ_coef, vir_coef, occ_energy, vir_energy):
    aux_count, ao_count = lax.axis_size("aux"), lax.axis_size("ao")
    odd = lax.axis_index("aux") % 2

    def place(block, parity):
        return block * ao_count + (parity ^ flipped(block))

    every = [(b, p) for b in range(aux_count) for p in range(ao_count)]

    def shifted(value, distance):
        route = [(place((b - distance) % aux_count, p), place(b, p)) for b, p in every]
        return lax.ppermute(value, BOTH, route)

    def across(value):
        return lax.ppermute(value, "aux", [(b ^ 1, b) for b in range(aux_count)])

    def over(value):
        return lax.ppermute(value, "ao", SWAP)

    hold = lax.optimization_barrier
    slots = [place(b, p) for b, p in every]
    vir_other = over(vir_coef)
    tiles = transform(ints, occ_coef, slots)
    arrived = lax.all_to_all(tiles, BOTH, split_axis=0, concat_axis=0, tiled=True)
    arrived = arrived.reshape(aux_count, ao_count, *arrived.shape[1:])
    arrived, vir_other = hold((arrived, vir_other))
    row = vir_energy[None, :]
    own, column = combine(arrived, vir_coef, vir_other, row)
    energies = (occ_energy, column, row)

    below, above = shifted(own, 2), shifted(own, -2)
    neighbour = across(own)
    own_pairs = [((0, 0), own), ((1, -1), neighbour)]
    mine, turned = add_pairs(energies, {}, [(*v, (0,)) for v in own_pairs], {}, turn=True)
    mine, turned_other = {0: mine}, over(turned)
    below, above, mine = hold((below, above, mine))
    far_below, far_above = shifted(below, 2), shifted(above, -2)
    next_below, next_above = across(below), across(above)

    turned_other, mine = hold((turned_other, mine))
    both = {0: turned, 1: turned_other}
    near = [((-2, -2), below), ((2, 2), above), ((-1, -3), next_below), ((3, 1), next_above)]
    plan = [(*v, (1,)) for v in own_pairs] + [(*v, (0, 1)) for v in near]
    density = add_pairs(energies, both, plan, mine)
    far_below, far_above, density = hold((far_below, far_above, density))

    remaining = across(jnp.where(odd == 0, far_above, far_below))
    far = [((-4, -4), far_below), ((4, 4), far_above)]
    final = [((-3, 3), remaining)]
    other = add_pairs(energies, {1: turned_other}, [(*v, (1,)) for v in far], {1: density[1]})
    remaining, other = hold((remaining, other))
    kept_other, sent = add_pairs(
        energies, {1: turned_other}, [(*v, (1,)) for v in final], other, last=1
    )
    came_own = over(sent)
    turned, sent = hold((turned, sent))
    kept_own, *sent = add_pairs(
        energies, {0: turned}, [(*v, (0,)) for v in far + final], {0: density[0]}, last=1
    )
    came_other = [over(piece) for piece in sent]
    output = finish(0, kept_own, [came_own], None)
    came_other, output = hold((came_other, output))
    return finish(1, kept_other, came_other, output)


def solution(mesh):
    return jax.shard_map(
        shards,
        mesh=mesh,
        in_specs=(P("aux", "ao", None), P(), P("ao", None), P(), P()),
        out_specs=P("aux", "ao", None),
        check_vma=False,
    )
```
